32 devices in a mesh: seq: 16 (over z, y, x), fsdp: 2 (over core).
Axes of the slice: x: 2, y: 2, z: 4, core: 2. Of those that a mesh axis runs over, the one named last changes fastest.
Arguments:
- queries: bfloat16 [2, 2048, 8192], P('fsdp', 'seq'), may hold values from -10 to 10
- keys: bfloat16 [2, 2048, 1024], P('fsdp', 'seq'), may hold values from -10 to 10
- values: bfloat16 [2, 2048, 1024], P('fsdp', 'seq'), may hold values from -6 to 6
- out_grad: bfloat16 [2, 2048, 8192], P('fsdp', 'seq'), may hold values from -6 to 6
- doc_lengths: int32 [2, 16], P('fsdp'), may hold values from 1 to 1024, 2048 in all within a row
- inputs: bfloat16 [2, 2048, 4096], P('fsdp', 'seq'), may hold values from -6 to 6
- value_weight: bfloat16 [4096, 1024], P('fsdp'), may hold values from -0.1875 to 0.1875
Outputs:
- grad_queries: bfloat16 [2, 2048, 8192], P('fsdp', 'seq')
- grad_keys: bfloat16 [2, 2048, 1024], P('fsdp', 'seq')
- grad_values: bfloat16 [2, 2048, 1024], P('fsdp', 'seq')
- grad_inputs: bfloat16 [2, 2048, 4096], P('fsdp', 'seq')
- grad_weight: float32 [4096, 1024], P(('seq', 'fsdp'))
The draws below stay inside these ranges and needn't reach their ends.
Inputs may be any that keep to these rules, and one draw needn't show every extreme that they name: `doc_lengths`: each row lists the lengths of the 16 documents packed into one sequence, in order; they sum to 2048 and the longest is exactly 1024.
All inputs are finite; a program needn't handle non-finite values.
Results may differ from the reference program's by a relative error of at most 0.0079.
Values may be sent and summed in bfloat16 or wider, within the bound.
No kernel may reach another device: no remote copies, remote signals or barrier semaphores. Data moves between devices by JAX's collectives and lax.ppermute only.
A program may use at most 192 MiB of HBM per device.

```python
import math
import jax
import jax.numpy as jnp
import numpy as np
from jax import lax

HEADS = 64
KV_HEADS = 8
HEAD_DIM = 128
DW = 4096
MAXDOC = 1024
SEQLEN = 2048
DOCS = 16
N_FSDP = 2


def drawn_pair(key):
    base = jax.random.fold_in(key, 7331)
    split_keys = jax.random.split(base, 2)
    shape_kv = (N_FSDP, SEQLEN, KV_HEADS, HEAD_DIM)
    query_draw = jnp.clip(jax.random.normal(split_keys[0], (N_FSDP, SEQLEN, HEADS, HEAD_DIM), jnp.float32), -6.0, 6.0)
    key_draw = jnp.clip(jax.random.normal(split_keys[1], shape_kv, jnp.float32), -6.0, 6.0)
    return (query_draw.reshape(N_FSDP, SEQLEN, HEADS * HEAD_DIM), key_draw.reshape(N_FSDP, SEQLEN, KV_HEADS * HEAD_DIM))


def draw_queries(key, part):
    return drawn_pair(key)[0].astype(jnp.bfloat16)


def draw_keys(key, part):
    return drawn_pair(key)[1].astype(jnp.bfloat16)


def spiked(array, own_key, source, target, parts, factor):
    def block_of(dim):
        return (jnp.arange(array.shape[dim]) // (array.shape[dim] // parts)).reshape((-1,) + (1,) * (array.ndim - 1 - dim))

    one_side = jax.random.permutation(own_key, parts)[block_of(target)]
    second = (block_of(target) + parts // 2) % parts
    return jnp.where((block_of(source) == one_side) | (block_of(source) == second), factor * array, array)


def steps_of(rng, dims, cuts, low, top_value):
    factor_of = 1.0
    for dim, blocks in cuts:
        heights = jax.random.uniform(jax.random.fold_in(jax.random.fold_in(rng, 6), dim), (blocks,), jnp.float32, low / len(cuts), top_value / len(cuts))
        factor_of = factor_of * jnp.repeat(jnp.exp(heights), dims[dim] // blocks).reshape((-1,) + (1,) * (len(dims) - 1 - dim))
    return factor_of


def length_profile(count, total, reach, slope):
    weights = [(1 << 20) // math.isqrt(grade ** slope) + 1 for grade in range(2, count + 1)]
    rest, given = total - reach - (count - 1), [1] * (count - 1)
    while rest > 0:
        candidates = [i for i in range(count - 1) if given[i] < reach]
        pool, remaining = sum([weights[i] for i in candidates]), rest
        for i in candidates:
            more = min(reach - given[i], max(1, remaining * weights[i] // pool), rest)
            given[i] = given[i] + more
            rest = rest - more
    return np.array([reach] + given)


def uneven_parts(key, count, total, reach, slope):
    if count == 2:
        one = jax.random.randint(key, (), max(1, total - reach), min(reach, total - 1) + 1)
        return jnp.stack([one, total - one])
    sizes = jnp.asarray(length_profile(count, total, reach, slope), jnp.int32)
    couples = (count - 1) // 2
    donor, taker = sizes[1:1 + 2 * couples:2], sizes[2:2 + 2 * couples:2]
    slack = jnp.minimum(donor - 1, reach - taker)
    shifted = jax.random.randint(jax.random.fold_in(key, 1), (couples,), 0, 1 << 20) % (slack + 1)
    sizes = sizes.at[1:1 + 2 * couples:2].set(donor - shifted).at[2:2 + 2 * couples:2].set(taker + shifted)
    return sizes[jax.random.permutation(jax.random.fold_in(key, 2), count)]


def centred(key, shape, deviation, most, pieces=(), held_as=jnp.bfloat16):
    loudness = steps_of(key, shape, pieces, -0.22, 0.18) if pieces else 1.0
    array = jax.random.normal(key, shape, jnp.float32) * deviation * loudness
    return jnp.minimum(jnp.maximum(array, -most), most).astype(held_as)


def heavy_noise(own_key, dims, scale, most, cuts, heavy, held_as=jnp.bfloat16):
    values = scale * jax.random.normal(own_key, dims, jnp.float32)
    if cuts:
        values = values * steps_of(own_key, dims, cuts, -0.22, 0.18)
    return jnp.clip(spiked(values, jax.random.fold_in(own_key, 3), *heavy), -most, most).astype(held_as)


def setup_inputs(seed: int = 0) -> dict:
    key_of = jax.random.split(jax.random.key(seed), 8)
    return {
        "queries": draw_queries(jax.random.fold_in(key_of[7], 71), 0),
        "keys": draw_keys(jax.random.fold_in(key_of[7], 71), 0),
        "values": centred(key_of[2], (N_FSDP, SEQLEN, KV_HEADS * HEAD_DIM), 1.0, 6.0, ((0, 2), (1, 16))),
        "out_grad": centred(key_of[3], (N_FSDP, SEQLEN, HEADS * HEAD_DIM), 1.0, 6.0, ((0, 2), (1, 16))),
        "doc_lengths": jax.vmap(lambda own: uneven_parts(own, DOCS, SEQLEN, MAXDOC, 2))(jax.random.split(key_of[4], N_FSDP)).reshape((N_FSDP, DOCS)).astype(jnp.int32),
        "inputs": heavy_noise(key_of[5], (N_FSDP, SEQLEN, DW), 1.0, 6.0, ((0, 2), (1, 16)), (1, 2, 16, 2.0)),
        "value_weight": centred(key_of[6], (DW, KV_HEADS * HEAD_DIM), (KV_HEADS * HEAD_DIM) ** -0.5, 0.1875, ((0, 2),)),
    }


masked_value = -1e+30

def document_ids(lengths, seqlen_value):
    bounds = jnp.cumsum(lengths).astype(jnp.int32)
    positions = jnp.arange(seqlen_value, dtype=jnp.int32)
    return lax.optimization_barrier(jnp.sum((positions[:, None] >= bounds[None, :]).astype(jnp.int32), axis=1)).astype(jnp.int32)

def head_backward(query_one, key_one, value_one, grad_one, doc_ids, block_rows, reach_back):
    seq_rows, head_width = query_one.shape
    score_scale = 1.0 / math.sqrt(head_width)
    slab_rows = block_rows + reach_back
    pad_keys = jnp.concatenate([jnp.zeros((reach_back, head_width), key_one.dtype), key_one], axis=0)
    pad_values = jnp.concatenate([jnp.zeros((reach_back, head_width), value_one.dtype), value_one], axis=0)
    pad_docs = jnp.concatenate([jnp.full((reach_back,), -1, jnp.int32), doc_ids], axis=0)
    query_offsets = jnp.arange(block_rows, dtype=jnp.int32)
    key_offsets = jnp.arange(slab_rows, dtype=jnp.int32)

    def visit(state_pair, offset):
        key_grad, value_grad = state_pair
        query_block = lax.dynamic_slice_in_dim(query_one, offset, block_rows, 0)
        grad_block = lax.dynamic_slice_in_dim(grad_one, offset, block_rows, 0)
        key_block = lax.dynamic_slice_in_dim(pad_keys, offset, slab_rows, 0)
        value_block = lax.dynamic_slice_in_dim(pad_values, offset, slab_rows, 0)
        query_docs = lax.dynamic_slice_in_dim(doc_ids, offset, block_rows, 0)
        key_docs = lax.dynamic_slice_in_dim(pad_docs, offset, slab_rows, 0)
        allowed = (query_docs[:, None] == key_docs[None, :]) & (key_offsets[None, :] <= query_offsets[:, None] + reach_back)
        scores = lax.dot_general(query_block, key_block, (((1,), (1,)), ((), ())), preferred_element_type=jnp.float32) * score_scale
        scores = jnp.where(allowed, scores, masked_value)
        row_max = lax.optimization_barrier(jnp.max(scores, axis=1, keepdims=True))
        weights = jnp.where(allowed, jnp.exp(scores - row_max), 0.0)
        probs = weights / lax.optimization_barrier(jnp.sum(weights, axis=1, keepdims=True))
        dprob = lax.dot_general(grad_block, value_block, (((1,), (1,)), ((), ())), preferred_element_type=jnp.float32)
        row_delta = lax.optimization_barrier(jnp.sum(probs * dprob, axis=1, keepdims=True))
        dscore = (probs * (dprob - row_delta)).astype(jnp.bfloat16)
        probs_low = probs.astype(jnp.bfloat16)
        query_grad = (jnp.dot(dscore, key_block, preferred_element_type=jnp.float32) * score_scale).astype(jnp.bfloat16)
        key_part = lax.dot_general(dscore, query_block, (((0,), (0,)), ((), ())), preferred_element_type=jnp.float32) * score_scale
        value_part = lax.dot_general(probs_low, grad_block, (((0,), (0,)), ((), ())), preferred_element_type=jnp.float32)
        key_grad = lax.dynamic_update_slice_in_dim(key_grad, lax.dynamic_slice_in_dim(key_grad, offset, slab_rows, 0) + key_part, offset, 0)
        value_grad = lax.dynamic_update_slice_in_dim(value_grad, lax.dynamic_slice_in_dim(value_grad, offset, slab_rows, 0) + value_part, offset, 0)
        return ((key_grad, value_grad), query_grad)
    empty_grads = jnp.zeros((seq_rows + reach_back, head_width), jnp.float32)
    offsets = jnp.arange(seq_rows // block_rows, dtype=jnp.int32) * block_rows
    (key_grad, value_grad), query_grads = lax.scan(visit, (empty_grads, empty_grads), offsets)
    return (query_grads.reshape(seq_rows, head_width), key_grad[reach_back:], value_grad[reach_back:])

def reference(queries, keys, values, out_grad, doc_lengths, inputs, value_weight):
    block_rows = min(512, SEQLEN)
    group_size = HEADS // KV_HEADS
    query_list, key_list, value_list, input_list = ([], [], [], [])
    weight_sum = jnp.zeros((DW, KV_HEADS * HEAD_DIM), jnp.float32)
    for sequence in range(N_FSDP):
        doc_ids = document_ids(doc_lengths[sequence], SEQLEN)
        query_seq = queries[sequence].reshape(SEQLEN, HEADS, HEAD_DIM)
        grad_seq = out_grad[sequence].reshape(SEQLEN, HEADS, HEAD_DIM)
        key_seq = keys[sequence].reshape(SEQLEN, KV_HEADS, HEAD_DIM)
        value_seq = values[sequence].reshape(SEQLEN, KV_HEADS, HEAD_DIM)

        def one_head(head_index):
            kv_index = head_index // group_size
            return head_backward(lax.dynamic_index_in_dim(query_seq, head_index, 1, keepdims=False), lax.dynamic_index_in_dim(key_seq, kv_index, 1, keepdims=False), lax.dynamic_index_in_dim(value_seq, kv_index, 1, keepdims=False), lax.dynamic_index_in_dim(grad_seq, head_index, 1, keepdims=False), doc_ids, block_rows, MAXDOC)
        query_grads, key_terms, value_terms = lax.map(one_head, jnp.arange(HEADS, dtype=jnp.int32))
        query_list.append(jnp.transpose(query_grads, (1, 0, 2)).reshape(SEQLEN, HEADS * HEAD_DIM))
        key_sum = key_terms.reshape(KV_HEADS, group_size, SEQLEN, HEAD_DIM).sum(axis=1).astype(jnp.bfloat16)
        value_sum = value_terms.reshape(KV_HEADS, group_size, SEQLEN, HEAD_DIM).sum(axis=1).astype(jnp.bfloat16)
        key_flat = jnp.transpose(key_sum, (1, 0, 2)).reshape(SEQLEN, KV_HEADS * HEAD_DIM)
        value_flat = jnp.transpose(value_sum, (1, 0, 2)).reshape(SEQLEN, KV_HEADS * HEAD_DIM)
        key_list.append(key_flat)
        value_list.append(value_flat)
        input_list.append(lax.dot_general(value_flat, value_weight, (((1,), (1,)), ((), ())), preferred_element_type=jnp.float32).astype(jnp.bfloat16))
        weight_sum = weight_sum + lax.dot_general(inputs[sequence], value_flat, (((0,), (0,)), ((), ())), preferred_element_type=jnp.float32)
    grad_weight = weight_sum * (1.0 / math.sqrt(N_FSDP * SEQLEN))
    return (jnp.stack(query_list), jnp.stack(key_list), jnp.stack(value_list), jnp.stack(input_list), grad_weight)
```

```python
import functools
import math

import jax
import jax.numpy as jnp
from jax import lax
from jax.experimental import pallas as pl
from jax.experimental.pallas import tpu as pltpu
from jax.sharding import PartitionSpec as P

HEADS = 64
KV_HEADS = 8
HEAD_DIM = 128
MAXDOC = 1024
GROUP = 4
MASKED = -1e30
F32 = jnp.float32
BF16 = jnp.bfloat16


def exchange(value, bit):
    length = lax.axis_size("seq")
    return lax.ppermute(value, "seq", [(i, i ^ bit) for i in range(length)])


def plane_shift(value, by):
    length = lax.axis_size("seq")
    step = by * GROUP
    pairs = [(i, i + step) for i in range(length) if 0 <= i + step < length]
    return lax.ppermute(value, "seq", pairs)


def plane_turn(value, by):
    length = lax.axis_size("seq")
    return lax.ppermute(value, "seq", [(i, (i + by * GROUP) % length) for i in range(length)])


def core_turn(value, by):
    length = lax.axis_size("fsdp")
    return lax.ppermute(value, "fsdp", [(i, (i + by) % length) for i in range(length)])


def dot(a, b, ca, cb):
    return lax.dot_general(a, b, (((ca,), (cb,)), ((), ())), preferred_element_type=F32)


def stack_heads(block_ref, out_ref, heads, width):
    for h in range(heads):
        out_ref[h * block_ref.shape[0] : (h + 1) * block_ref.shape[0], :] = block_ref[
            :, h * width : (h + 1) * width
        ]


def fill_slots(pieces, order, slots):
    own, far, first, second, first_far, second_far = pieces
    rows = own.shape[0]
    one, two, three = order

    def put(plane, slot, value):
        at = (slot % 2) * rows
        slots[plane * 2 + slot // 2, at : at + rows, :] = value

    put(0, 0, own[...])
    put(0, one, first[...])
    put(0, two, second[0])
    put(0, three, second[1])
    for n in range(far.shape[0]):
        put(n + 1, 0, far[n])
        put(n + 1, one, first_far[n])
        put(n + 1, two, second_far[0, n])
        put(n + 1, three, second_far[1, n])


def tiled(block, times):
    return jnp.concatenate([block] * times, axis=1)


def value_kernel(
    order, heads, factor, flags, q_ref, g_ref, own, far, first, second, first_far, second_far,
    bias_ref, near_ref, away_ref, lse_ref, qs, gs, ks, score, top_ref, sum_ref,
):
    rows, width = own.shape
    pairs = ks.shape[0]
    stack_heads(q_ref, qs, heads, width)
    stack_heads(g_ref, gs, heads, width)
    fill_slots((own, far, first, second, first_far, second_far), order, ks)
    top_ref[...] = jnp.full(top_ref.shape, MASKED, F32)
    sum_ref[...] = jnp.zeros(sum_ref.shape, F32)

    @pl.loop(0, pairs)
    def _(j):
        @pl.when(flags[j] != 0)
        def _():
            s = dot(ks[j], qs[...], 1, 1) * factor + tiled(bias_ref[j], heads)
            score[j] = s
            top_ref[...] = jnp.maximum(top_ref[...], jnp.max(s.reshape(-1, 8, s.shape[1]), axis=0))

    top = jnp.max(top_ref[...], axis=0, keepdims=True)

    @pl.loop(0, pairs)
    def _(j):
        @pl.when(flags[j] != 0)
        def _():
            p = jnp.exp2(score[j] - top)
            score[j] = p
            sum_ref[...] = sum_ref[...] + jnp.sum(p.reshape(-1, 8, p.shape[1]), axis=0)

    total = jnp.sum(sum_ref[...], axis=0, keepdims=True)
    lse_ref[0] = top + jnp.log2(total)
    scale = 1.0 / total

    @pl.loop(0, pairs // 2)
    def _(plane):
        for side in range(2):
            j = plane * 2 + side

            def store(value, half):
                if order[0] == 1:
                    (near_ref, away_ref)[side][plane, half] = value
                else:
                    (near_ref, away_ref)[half][plane, side] = value

            @pl.when(flags[j] != 0)
            def _():
                out = dot((score[j] * scale).astype(BF16), gs[...], 1, 0).astype(BF16)
                store(out[:rows], 0)
                store(out[rows:], 1)

            @pl.when(flags[j] == 0)
            def _():
                blank = jnp.zeros((rows, width), BF16)
                store(blank, 0)
                store(blank, 1)


def key_kernel(
    order, heads, factor, scale, flags, q_ref, g_ref,
    k_own, k_far, k_first, k_second, k_first_far, k_second_far,
    v_own, v_far, v_first, v_second, v_first_far, v_second_far,
    bias_ref, lse_ref, dq_in, near_ref, away_ref, dq_ref,
    qs, gs, ks, vs, prob, dprob, sum_ref, dq_acc,
):
    del dq_in
    rows, width = k_own.shape
    pairs = ks.shape[0]
    stack_heads(q_ref, qs, heads, width)
    stack_heads(g_ref, gs, heads, width)
    fill_slots((k_own, k_far, k_first, k_second, k_first_far, k_second_far), order, ks)
    fill_slots((v_own, v_far, v_first, v_second, v_first_far, v_second_far), order, vs)
    sum_ref[...] = jnp.zeros(sum_ref.shape, F32)
    dq_acc[...] = jnp.zeros(dq_acc.shape, F32)
    lse = lse_ref[0]

    @pl.loop(0, pairs)
    def _(j):
        @pl.when(flags[j] != 0)
        def _():
            s = dot(ks[j], qs[...], 1, 1) * factor + tiled(bias_ref[j], heads)
            p = jnp.exp2(s - lse)
            dp = dot(vs[j], gs[...], 1, 1)
            prob[j] = p
            dprob[j] = dp
            pd = p * dp
            sum_ref[...] = sum_ref[...] + jnp.sum(pd.reshape(-1, 8, pd.shape[1]), axis=0)

    delta = jnp.sum(sum_ref[...], axis=0, keepdims=True)

    @pl.loop(0, pairs // 2)
    def _(plane):
        for side in range(2):
            j = plane * 2 + side

            def store(value, half):
                if order[0] == 1:
                    (near_ref, away_ref)[side][plane, half] = value
                else:
                    (near_ref, away_ref)[half][plane, side] = value

            @pl.when(flags[j] != 0)
            def _():
                ds = (prob[j] * (dprob[j] - delta)).astype(BF16)
                out = (dot(ds, qs[...], 1, 0) * scale).astype(BF16)
                store(out[:rows], 0)
                store(out[rows:], 1)
                dq_acc[...] += dot(ks[j], ds, 0, 0)

            @pl.when(flags[j] == 0)
            def _():
                blank = jnp.zeros((rows, width), BF16)
                store(blank, 0)
                store(blank, 1)

    for h in range(heads):
        part = dq_acc[:, h * rows : (h + 1) * rows] * scale
        dq_ref[:, h * width : (h + 1) * width] = part.T.astype(BF16)


def piece_specs(half_groups, offset, tok_rows, far_planes):
    wide = HEAD_DIM
    return [
        pl.BlockSpec((tok_rows, wide), lambda g, f: (0, g + offset)),
        pl.BlockSpec((far_planes, tok_rows, wide), lambda g, f: (0, 0, g + offset)),
        pl.BlockSpec((tok_rows, wide), lambda g, f: (0, g)),
        pl.BlockSpec((2, tok_rows, wide), lambda g, f: (0, 0, g)),
        pl.BlockSpec((far_planes, tok_rows, wide), lambda g, f: (0, 0, g)),
        pl.BlockSpec((2, far_planes, tok_rows, wide), lambda g, f: (0, 0, 0, g)),
    ]


def value_call(half, order, flags, queries, grads, pieces, bias):
    tok_rows = queries.shape[0]
    group_size = HEADS // KV_HEADS
    half_groups = KV_HEADS // 2
    offset = half * half_groups
    pairs = bias.shape[0]
    planes = pairs // 2
    wide = group_size * HEAD_DIM
    span = group_size * tok_rows
    factor = math.log2(math.e) / math.sqrt(HEAD_DIM)
    head_spec = pl.BlockSpec((tok_rows, wide), lambda g, f: (0, g + offset))
    part = jax.ShapeDtypeStruct((planes, 2, tok_rows, half_groups * HEAD_DIM), BF16)
    part_spec = pl.BlockSpec((planes, 2, tok_rows, HEAD_DIM), lambda g, f: (0, 0, 0, g))
    return pl.pallas_call(
        functools.partial(value_kernel, order, group_size, factor),
        grid_spec=pltpu.PrefetchScalarGridSpec(
            num_scalar_prefetch=1,
            grid=(half_groups,),
            in_specs=[head_spec, head_spec]
            + piece_specs(half_groups, offset, tok_rows, planes - 1)
            + [pl.BlockSpec(bias.shape, lambda g, f: (0, 0, 0))],
            out_specs=[part_spec, part_spec, pl.BlockSpec((1, 1, span), lambda g, f: (g, 0, 0))],
            scratch_shapes=[
                pltpu.VMEM((span, HEAD_DIM), BF16),
                pltpu.VMEM((span, HEAD_DIM), BF16),
                pltpu.VMEM((pairs, 2 * tok_rows, HEAD_DIM), BF16),
                pltpu.VMEM((pairs, 2 * tok_rows, span), F32),
                pltpu.VMEM((8, span), F32),
                pltpu.VMEM((8, span), F32),
            ],
        ),
        out_shape=[part, part, jax.ShapeDtypeStruct((half_groups, 1, span), F32)],
        name=f"value_parts_{half}",
    )(flags, queries, grads, *pieces, bias)


def key_call(half, order, flags, queries, grads, k_pieces, v_pieces, bias, lse, dq):
    tok_rows = queries.shape[0]
    group_size = HEADS // KV_HEADS
    half_groups = KV_HEADS // 2
    offset = half * half_groups
    pairs = bias.shape[0]
    planes = pairs // 2
    wide = group_size * HEAD_DIM
    span = group_size * tok_rows
    scale = 1.0 / math.sqrt(HEAD_DIM)
    factor = math.log2(math.e) * scale
    head_spec = pl.BlockSpec((tok_rows, wide), lambda g, f: (0, g + offset))
    part = jax.ShapeDtypeStruct((planes, 2, tok_rows, half_groups * HEAD_DIM), BF16)
    part_spec = pl.BlockSpec((planes, 2, tok_rows, HEAD_DIM), lambda g, f: (0, 0, 0, g))
    specs = piece_specs(half_groups, offset, tok_rows, planes - 1)
    operands = [queries, grads, *k_pieces, *v_pieces, bias, lse, dq]
    return pl.pallas_call(
        functools.partial(key_kernel, order, group_size, factor, scale),
        grid_spec=pltpu.PrefetchScalarGridSpec(
            num_scalar_prefetch=1,
            grid=(half_groups,),
            in_specs=[head_spec, head_spec]
            + specs
            + specs
            + [
                pl.BlockSpec(bias.shape, lambda g, f: (0, 0, 0)),
                pl.BlockSpec((1, 1, span), lambda g, f: (g, 0, 0)),
                pl.BlockSpec(memory_space=pl.ANY),
            ],
            out_specs=[part_spec, part_spec, head_spec],
            scratch_shapes=[
                pltpu.VMEM((span, HEAD_DIM), BF16),
                pltpu.VMEM((span, HEAD_DIM), BF16),
                pltpu.VMEM((pairs, 2 * tok_rows, HEAD_DIM), BF16),
                pltpu.VMEM((pairs, 2 * tok_rows, HEAD_DIM), BF16),
                pltpu.VMEM((pairs, 2 * tok_rows, span), F32),
                pltpu.VMEM((pairs, 2 * tok_rows, span), F32),
                pltpu.VMEM((8, span), F32),
                pltpu.VMEM((HEAD_DIM, span), F32),
            ],
        ),
        out_shape=[part, part, jax.ShapeDtypeStruct(queries.shape, BF16)],
        input_output_aliases={len(operands): 2},
        name=f"key_parts_{half}",
    )(flags, *operands)


def weight_kernel(order, planes, places, x_ref, own, first, second, own_b, first_b, second_b, out_ref, xs):
    rows = x_ref.shape[1]
    for slot in range(GROUP):
        for n in range(planes):
            at = (slot * planes + n) * rows
            xs[at : at + rows, :] = x_ref[places[slot * planes + n]]
    span = planes * rows
    half = own.shape[1]
    for side, (a, b, c) in enumerate(((own, first, second), (own_b, first_b, second_b))):
        one, two, three = order[side]
        total = None
        for slot, ref in ((0, a[...]), (one, b[...]), (two, c[0]), (three, c[1])):
            part = dot(xs[slot * span : (slot + 1) * span, :], ref, 0, 0)
            total = part if total is None else total + part
        out_ref[:, side * half : (side + 1) * half] = total


ORDERS = ((1, 2, 3), (2, 1, 3))


def spread(value, order):
    first = exchange(value, order[0])
    second = exchange(jnp.stack((value, first)), order[1])
    return first, second


def window_pieces(own):
    tok_rows, columns = own.shape
    far_planes = -(-MAXDOC // (GROUP * tok_rows))
    shifted, current = [], own
    for _ in range(far_planes):
        current = plane_shift(current, 1)
        shifted.append(current)
    far = jnp.stack(shifted)
    half = columns // 2
    out = []
    for side in range(2):
        cols = slice(side * half, (side + 1) * half)
        first, second = spread(own[:, cols], ORDERS[side])
        first_far, second_far = spread(far[:, :, cols], ORDERS[side])
        out.append((own, far, first, second, first_far, second_far))
    return out


def add(a, b):
    return a.astype(F32) + b.astype(F32)


def collect(parts):
    sums = []
    for side in range(2):
        near, away = parts[side]
        order = ORDERS[side]
        near = add(near, exchange(away, order[1])).astype(BF16)
        sums.append(add(near[:, 0], exchange(near[:, 1], order[0])).astype(BF16))
    total = jnp.concatenate(sums, axis=2)
    planes = total.shape[0]
    carried = total[planes - 1]
    for n in range(planes - 2, 0, -1):
        carried = add(plane_shift(carried, -1), total[n]).astype(BF16)
    return add(plane_shift(carried, -1), total[0]).astype(BF16)


def local(queries, keys, values, out_grad, doc_lengths, inputs, value_weight):
    seq_count = lax.axis_size("seq")
    fsdp_count = lax.axis_size("fsdp")
    tok_rows = queries.shape[1]
    planes_all = seq_count // GROUP
    me = lax.axis_index("seq")
    core = lax.axis_index("fsdp")
    plane, place = me // GROUP, me % GROUP
    query_local, grad_local = queries[0], out_grad[0]

    moved = lax.all_to_all(
        inputs[0].reshape(tok_rows, seq_count, -1), "seq", split_axis=1, concat_axis=0, tiled=False
    )
    weights = [value_weight] + [core_turn(value_weight, d) for d in range(1, fsdp_count)]

    far_planes = -(-MAXDOC // (GROUP * tok_rows))
    slots = jnp.arange(GROUP, dtype=jnp.int32)
    places = jnp.bitwise_xor(slots, place)
    blocks = (plane - jnp.arange(far_planes + 1, dtype=jnp.int32))[:, None] * GROUP + places[None]
    offsets = jnp.arange(tok_rows, dtype=jnp.int32)
    key_at = (blocks[:, :, None] * tok_rows + offsets).reshape(-1)
    query_at = me * tok_rows + offsets
    lengths = doc_lengths[0]
    number = jnp.arange(lengths.shape[0], dtype=jnp.int32)
    bounds = jnp.sum(jnp.where(number[:, None] <= number[None], lengths[:, None], 0), axis=0)

    def documents(positions):
        return jnp.sum((positions[:, None] >= bounds[None]).astype(jnp.int32), axis=1)

    allowed = (
        (documents(key_at)[:, None] == documents(query_at)[None])
        & (key_at[:, None] <= query_at[None])
        & (key_at[:, None] >= 0)
    ).reshape(-1, 2 * tok_rows, tok_rows)
    bias = jnp.where(allowed, 0.0, MASKED).astype(F32)
    flags = jnp.any(allowed, axis=(1, 2)).astype(jnp.int32)

    k_pieces = window_pieces(keys[0])
    v_pieces = window_pieces(values[0])

    value_parts, stats = [], []
    for side in range(2):
        near, away, lse = value_call(
            side, ORDERS[side], flags, query_local, grad_local, k_pieces[side], bias
        )
        value_parts.append((near, away))
        stats.append(lse)
    value_flat = collect(value_parts)

    key_parts = []
    query_back = jnp.zeros(query_local.shape, BF16)
    for side in range(2):
        near, away, query_back = key_call(
            side, ORDERS[side], flags, query_local, grad_local, k_pieces[side], v_pieces[side],
            bias, stats[side], query_back,
        )
        key_parts.append((near, away))
    key_flat = collect(key_parts)

    own_rows = value_weight.shape[0]
    grad_in = jnp.zeros((tok_rows, own_rows * fsdp_count), BF16)
    for d, weight in enumerate(weights):
        piece = dot(value_flat, weight, 1, 1).astype(BF16)
        at = ((core - d) % fsdp_count) * own_rows
        grad_in = lax.dynamic_update_slice_in_dim(grad_in, piece, at, 1)

    column = jnp.stack([value_flat] + [plane_turn(value_flat, d) for d in range(1, planes_all)])
    half = value_flat.shape[1] // 2
    span = planes_all * tok_rows
    operands = []
    for side in range(2):
        mine = column[:, :, side * half : (side + 1) * half]
        first, second = spread(mine, ORDERS[side])
        operands += [mine.reshape(span, half), first.reshape(span, half), second.reshape(2, span, half)]
    sources = (
        ((plane - jnp.arange(planes_all, dtype=jnp.int32)) % planes_all)[None] * GROUP
        + places[:, None]
    ).reshape(-1)
    share = moved.shape[2]
    grad_w = pl.pallas_call(
        functools.partial(weight_kernel, ORDERS, planes_all),
        in_specs=[pl.BlockSpec(memory_space=pltpu.SMEM)]
        + [pl.BlockSpec(memory_space=pltpu.VMEM)] * 7,
        out_specs=pl.BlockSpec(memory_space=pltpu.VMEM),
        out_shape=jax.ShapeDtypeStruct((share, 2 * half), F32),
        scratch_shapes=[pltpu.VMEM((seq_count * tok_rows, share), BF16)],
        name="weight_parts",
    )(sources, moved, *operands)
    rows = share // fsdp_count
    grad_w = grad_w.reshape(fsdp_count, rows, -1)
    total = lax.dynamic_index_in_dim(grad_w, core, 0, keepdims=False)
    for d in range(1, fsdp_count):
        sent = lax.dynamic_index_in_dim(grad_w, (core + d) % fsdp_count, 0, keepdims=False)
        total = total + core_turn(sent, d)
    weight_scale = 1.0 / math.sqrt(tok_rows * seq_count * fsdp_count)
    return (query_back[None], key_flat[None], value_flat[None], grad_in[None], total * weight_scale)


def solution(mesh):
    tokens = P("fsdp", "seq", None)
    in_specs = (tokens, tokens, tokens, tokens, P("fsdp", None), tokens, P("fsdp", None))
    out_specs = (tokens, tokens, tokens, tokens, P(("seq", "fsdp"), None))
    return jax.shard_map(local, mesh=mesh, in_specs=in_specs, out_specs=out_specs, check_vma=False)
```
